256 devices in a mesh: pipe: 4 (over x), expert: 16 (over z, core), dp: 4 (over y).
Axes of the slice: x: 4, y: 4, z: 8, core: 2. Of those that a mesh axis runs over, the one named last changes fastest.
Arguments:
- tokens: bfloat16 [4, 8192, 2048], P('pipe', ('expert', 'dp')), may hold values from -6 to 6
- cotangent: bfloat16 [4, 8192, 2048], P('pipe', ('expert', 'dp')), may hold values from -6 to 6
- norm_gain: float32 [4, 2048], P('pipe'), may hold values from 0.5 to 1.5
- first_ids: int32 [4, 8192, 2], P('pipe', ('expert', 'dp')), may hold values from 0 to 7, all different within a row; in each aligned block of 128 rows (0 to 127, 128 to 255, ..., all dimensions but the last counted through in order) at most 36 rows name the same one
- first_gates: float32 [4, 8192, 2], P('pipe', ('expert', 'dp')), may hold values from 0.1 to 1
- second_ids: int32 [4, 8192, 2], P('pipe', ('expert', 'dp')), may hold values from 0 to 7, all different within a row; in each aligned block of 128 rows (0 to 127, 128 to 255, ..., all dimensions but the last counted through in order) at most 36 rows name the same one
- second_gates: float32 [4, 8192, 2], P('pipe', ('expert', 'dp')), may hold values from 0.1 to 1
- new_slot: int32 [4, 8], P('pipe'), may hold values from 0 to 7, each once within a row
- inner_weight: float32 [4, 16, 2, 2048, 384], P('pipe', 'expert', None, 'dp'), may hold values from -0.125 to 0.125
- outer_weight: float32 [4, 16, 384, 2048], P('pipe', 'expert', None, 'dp'), may hold values from -0.21875 to 0.21875
- inner_mean: bfloat16 [4, 16, 2, 2048, 384], P('pipe', 'expert', None, 'dp'), may hold values from -60 to 60
- outer_mean: bfloat16 [4, 16, 384, 2048], P('pipe', 'expert', None, 'dp'), may hold values from -60 to 60
- inner_square: bfloat16 [4, 16, 2, 2048, 384], P('pipe', 'expert', None, 'dp'), may hold values from 10 to 1000
- outer_square: bfloat16 [4, 16, 384, 2048], P('pipe', 'expert', None, 'dp'), may hold values from 10 to 1000
Outputs:
- layer_out: bfloat16 [4, 8192, 2048], P('pipe', ('expert', 'dp'))
- weight_inner: float32 [4, 16, 2, 2048, 384], P('pipe', 'expert', None, 'dp')
- weight_outer: float32 [4, 16, 384, 2048], P('pipe', 'expert', None, 'dp')
- mean_inner: bfloat16 [4, 16, 2, 2048, 384], P('pipe', 'expert', None, 'dp')
- mean_outer: bfloat16 [4, 16, 384, 2048], P('pipe', 'expert', None, 'dp')
- square_inner: bfloat16 [4, 16, 2, 2048, 384], P('pipe', 'expert', None, 'dp')
- square_outer: bfloat16 [4, 16, 384, 2048], P('pipe', 'expert', None, 'dp')
The draws below stay inside these ranges and needn't reach their ends.
Inputs may be any that keep to these rules, and one draw needn't show every extreme that they name: `first_ids`: each token names 2 different experts. Within the rows of one device no expert is named more than 36 times, and some device names some expert exactly 36 times. `second_ids`: as first_ids. `new_slot`: for each section, a permutation of the 8 experts.
All inputs are finite; a program needn't handle non-finite values.
Results may differ from the reference program's by a relative error of at most 0.008.
Values may be sent and summed in bfloat16 or wider, within the bound.
No kernel may reach another device: no remote copies, remote signals or barrier semaphores. Data moves between devices by JAX's collectives and lax.ppermute only.
A program may use at most 128 MiB of HBM per device.

```python
import math
import jax
import jax.numpy as jnp
import numpy as np
from jax import lax

D = 2048
FF = 768
TOK_DEV = 128
EXPERTS = 8
TOPK = 2
CAP = 36
TOKENS = 8192
N_PIPE = 4
N_EXPERT = 16
N_DP = 4


def shard_levels(stream_key, extent, shards, least, largest):
    loudness, own = 1.0, jax.random.fold_in(stream_key, 6)
    for dim, shards_of in shards:
        draws = jnp.exp(jax.random.uniform(jax.random.fold_in(own, dim), (shards_of,), jnp.float32, least / len(shards), largest / len(shards)))
        loudness = loudness * jnp.repeat(draws, extent[dim] // shards_of).reshape([-1 if axis == dim else 1 for axis in range(len(extent))])
    return loudness


def routed_block(key, own, number, rows, count, top, reach, lean):
    sequence = jax.random.permutation(key, count)
    packed, ordinary = load_shares(count, rows * top, reach, lean, True), load_shares(count, rows * top, reach, lean, False)
    places = jnp.arange(count)

    def named(lengths, offset_by):
        used = int((lengths > 0).sum())
        fixed = max(1, used // 4)
        passed = fixed + (places - fixed + offset_by * (used - fixed)) % max(1, count - fixed)
        return jnp.zeros((count,), jnp.int32).at[sequence[jnp.where(places < fixed, places, passed)]].set(jnp.asarray(lengths, jnp.int32))

    lengths = jnp.where(number % 4 == 0, named(packed, number // 4), named(ordinary, number - number // 4 - 1))
    mixed = jax.random.permutation(jax.random.fold_in(own, 3), count)
    source_of, sink = mixed[0:count // 2 * 2:2], mixed[1:count // 2 * 2:2]
    margin = jnp.minimum(lengths[source_of] - 1, reach - lengths[sink]) // 2
    margin = jnp.where((source_of == sequence[0]) | (sink == sequence[0]) | (lengths[sink] == 0), 0, jnp.maximum(margin, 0))
    passed = jax.random.randint(jax.random.fold_in(own, 4), (count // 2,), 0, 1 << 20) % (margin + 1)
    lengths = lengths.at[source_of].add(-passed).at[sink].add(passed)
    items = jnp.searchsorted(jnp.cumsum(lengths), jnp.arange(rows * top), side="right").astype(jnp.int32)
    listing = items.reshape(top, rows).T
    listing = listing[jax.random.permutation(jax.random.fold_in(own, 1), rows)]
    offset_by = jax.random.randint(jax.random.fold_in(own, 2), (rows, 1), 0, top)
    return jnp.take_along_axis(listing, (jnp.arange(top)[None, :] + offset_by) % top, axis=1)


def load_shares(amount, total, bound, lean, full):
    portions = [(1 << 20) // math.isqrt(grade ** lean) + 1 for grade in range(1, amount + 1)]
    largest = bound if full else min(bound, max(-(-total // amount), total * portions[0] // sum(portions)))
    least = 1 if total - largest >= amount - 1 else 0
    given, rest = [largest] + [least] * (amount - 1), total - largest - least * (amount - 1)
    while rest > 0:
        movable = [i for i in range(1, amount) if given[i] < largest] or [i for i in range(1, amount) if given[i] < bound]
        mass, left = sum([portions[i] for i in movable]), rest
        for i in movable:
            more = min(bound - given[i], max(1, left * portions[i] // mass), rest)
            given[i] = given[i] + more
            rest = rest - more
    return np.array(given)


def centred(rng, extent, spread, bound, shards=(), held_as=jnp.bfloat16):
    entries = spread * jax.random.normal(rng, extent, jnp.float32)
    if shards:
        entries = entries * shard_levels(rng, extent, shards, -0.22, 0.18)
    return jnp.clip(entries, -bound, bound).astype(held_as)


def setup_inputs(seed: int = 0) -> dict:
    arg_keys = jax.random.split(jax.random.key(seed), 15)
    tokens = centred(arg_keys[0], (N_PIPE, TOKENS, D), 1.0, 6.0, ((0, 4), (1, 64)))
    cotangent = centred(arg_keys[1], (N_PIPE, TOKENS, D), 1.0, 6.0, ((0, 4), (1, 64)))
    norm_gain = jnp.clip(1.0 + 0.1 * jax.random.normal(arg_keys[2], (N_PIPE, D), jnp.float32), 0.5, 1.5)
    first_ids_keys = jax.random.split(jax.random.fold_in(arg_keys[3], 1), N_PIPE * TOKENS // TOK_DEV)
    first_ids_turns = jax.random.permutation(jax.random.fold_in(arg_keys[3], 3), N_PIPE * TOKENS // TOK_DEV)
    first_ids = jax.vmap(lambda own, number: routed_block(jax.random.fold_in(arg_keys[3], 2), own, number, TOK_DEV, EXPERTS, TOPK, CAP, 1))(first_ids_keys, first_ids_turns).reshape((N_PIPE, TOKENS, TOPK))
    first_gates = jnp.clip(0.1 + 0.9 * jax.random.uniform(arg_keys[4], (N_PIPE, TOKENS, TOPK), jnp.float32) ** shard_levels(arg_keys[4], (N_PIPE, TOKENS, TOPK), ((0, 4), (1, 64)), -0.2, 0.2), 0.1, 1.0)
    second_ids_keys = jax.random.split(jax.random.fold_in(arg_keys[5], 1), N_PIPE * TOKENS // TOK_DEV)
    second_ids_turns = jax.random.permutation(jax.random.fold_in(arg_keys[5], 3), N_PIPE * TOKENS // TOK_DEV)
    second_ids = jax.vmap(lambda own, number: routed_block(jax.random.fold_in(arg_keys[5], 2), own, number, TOK_DEV, EXPERTS, TOPK, CAP, 1))(second_ids_keys, second_ids_turns).reshape((N_PIPE, TOKENS, TOPK))
    second_gates = jnp.clip(0.1 + 0.9 * jax.random.uniform(arg_keys[6], (N_PIPE, TOKENS, TOPK), jnp.float32) ** shard_levels(arg_keys[6], (N_PIPE, TOKENS, TOPK), ((0, 4), (1, 64)), -0.2, 0.2), 0.1, 1.0)
    new_slot = jax.vmap(lambda own: jax.random.permutation(own, EXPERTS))(jax.random.split(arg_keys[7], N_PIPE)).reshape((N_PIPE, EXPERTS)).astype(jnp.int32)
    inner_weight = centred(arg_keys[8], (N_PIPE, 2 * EXPERTS, 2, D, FF // 2), D ** -0.5, 0.125, ((0, 4), (1, 16), (3, 4)), jnp.float32)
    outer_weight = centred(arg_keys[9], (N_PIPE, 2 * EXPERTS, FF // 2, D), FF ** -0.5, 0.21875, ((0, 4), (1, 16), (3, 4)), jnp.float32)
    inner_mean = centred(arg_keys[10], (N_PIPE, 2 * EXPERTS, 2, D, FF // 2), 10.0, 60.0, ((0, 4), (1, 16), (3, 4)))
    outer_mean = centred(arg_keys[11], (N_PIPE, 2 * EXPERTS, FF // 2, D), 10.0, 60.0, ((0, 4), (1, 16), (3, 4)))
    inner_square = jnp.clip(jnp.exp(math.log(1000.0) - 4.6051702 * jax.random.uniform(arg_keys[12], (N_PIPE, 2 * EXPERTS, 2, D, FF // 2), jnp.float32) ** shard_levels(arg_keys[12], (N_PIPE, 2 * EXPERTS, 2, D, FF // 2), ((0, 4), (1, 16), (3, 4)), -0.2, 0.2)), 10.0, 1000.0).astype(jnp.bfloat16)
    outer_square = jnp.clip(jnp.exp(math.log(1000.0) - 4.6051702 * jax.random.uniform(arg_keys[13], (N_PIPE, 2 * EXPERTS, FF // 2, D), jnp.float32) ** shard_levels(arg_keys[13], (N_PIPE, 2 * EXPERTS, FF // 2, D), ((0, 4), (1, 16), (3, 4)), -0.2, 0.2)), 10.0, 1000.0).astype(jnp.bfloat16)
    return {"tokens": tokens, "cotangent": cotangent, "norm_gain": norm_gain, "first_ids": first_ids, "first_gates": first_gates, "second_ids": second_ids, "second_gates": second_gates, "new_slot": new_slot, "inner_weight": inner_weight, "outer_weight": outer_weight, "inner_mean": inner_mean, "outer_mean": outer_mean, "inner_square": inner_square, "outer_square": outer_square}


norm_eps = 1e-06
learn_rate = 0.001
beta_one = 0.9
beta_two = 0.95
adam_eps = 1e-08
bias_one = 0.999973438601112
bias_two = 0.994079470779667

def normed(values, gain_row):
    widened = values.astype(jnp.float32)
    inverse_rms = lax.rsqrt(lax.optimization_barrier(jnp.mean(widened * widened, axis=-1, keepdims=True)) + norm_eps)
    return (widened * inverse_rms * gain_row).astype(jnp.bfloat16)

def silu_parts(gate_proj):
    logistic = jax.nn.sigmoid(gate_proj)
    return (gate_proj * logistic, logistic * (1.0 + gate_proj * (1.0 - logistic)))

def half_forward(token_rows, inner_full, outer_full):
    gate_proj = jnp.dot(token_rows, inner_full[0], preferred_element_type=jnp.float32)
    up_proj = jnp.dot(token_rows, inner_full[1], preferred_element_type=jnp.float32)
    activity = (silu_parts(gate_proj)[0] * up_proj).astype(jnp.bfloat16)
    half_out = jnp.dot(activity, outer_full, preferred_element_type=jnp.float32).astype(jnp.bfloat16)
    return (half_out, activity, gate_proj, up_proj)

def half_backward(token_rows, grad_rows, outer_full, activity, gate_proj, up_proj):
    grad_outer = jnp.dot(activity.T, grad_rows, preferred_element_type=jnp.float32)
    d_active = jnp.dot(grad_rows, outer_full.T, preferred_element_type=jnp.float32)
    swish_value, swish_slope = silu_parts(gate_proj)
    d_gate = (d_active * up_proj * swish_slope).astype(jnp.bfloat16)
    d_upper = (d_active * swish_value).astype(jnp.bfloat16)
    grad_gate = jnp.dot(token_rows.T, d_gate, preferred_element_type=jnp.float32)
    grad_upper = jnp.dot(token_rows.T, d_upper, preferred_element_type=jnp.float32)
    return (jnp.stack([grad_gate, grad_upper]), grad_outer)

def slot_rows(ids):
    blocked = ids.reshape(-1, TOK_DEV * TOPK)
    onehot = (blocked[..., None] == jnp.arange(EXPERTS, dtype=jnp.int32)).astype(jnp.int32)
    ranking = lax.optimization_barrier(jnp.sum((jnp.cumsum(onehot, axis=1) - 1) * onehot, axis=2)).astype(jnp.int32)
    starts = jnp.arange(blocked.shape[0], dtype=jnp.int32)[:, None] * CAP
    return (starts + ranking).reshape(ids.shape).astype(jnp.int32)

def scatter_rows(values, ids, positions):
    buffer = jnp.zeros((EXPERTS, TOKENS // TOK_DEV * CAP, D), jnp.bfloat16)
    return buffer.at[ids, positions].set(values)

def section_forward(token_rows, gain_row, ids, gates, inner_low, outer_low):
    normal = normed(token_rows, gain_row)
    positions = slot_rows(ids)
    buffer = scatter_rows(jnp.broadcast_to(normal[:, None, :], ids.shape + (D,)), ids, positions)
    totals = []
    stored = []
    for expert in range(EXPERTS):
        summed = jnp.zeros((buffer.shape[1], D), jnp.float32)
        for half_index in range(2):
            slot = 2 * expert + half_index
            half_out, activity, gate_proj, up_proj = half_forward(buffer[expert], inner_low[slot], outer_low[slot])
            summed = summed + lax.optimization_barrier(half_out).astype(jnp.float32)
            stored.append((activity, gate_proj, up_proj))
        totals.append(summed)
    totals = jnp.stack(totals)
    picked = totals[ids, positions]
    mixed_rows = token_rows.astype(jnp.float32) + lax.optimization_barrier(jnp.sum(gates[..., None] * picked, axis=1))
    return (mixed_rows.astype(jnp.bfloat16), buffer, stored)

def group_rows(values, dp_group):
    return values.reshape(N_EXPERT, N_DP, CAP, values.shape[-1])[:, dp_group].reshape(-1, values.shape[-1])

def section_grads(buffer, stored, grad_out, ids, gates, outer_low):
    positions = slot_rows(ids)
    grad_rows = (gates[..., None] * grad_out.astype(jnp.float32)[:, None, :]).astype(jnp.bfloat16)
    grad_buffer = scatter_rows(grad_rows, ids, positions)
    inner_list = []
    outer_list = []
    for expert in range(EXPERTS):
        for half_index in range(2):
            slot = 2 * expert + half_index
            activity, gate_proj, up_proj = stored[slot]
            total_inner = jnp.zeros((2, D, FF // 2), jnp.float32)
            total_outer = jnp.zeros((FF // 2, D), jnp.float32)
            for dp_group in range(N_DP):
                grad_inner, grad_outer = half_backward(group_rows(buffer[expert], dp_group), group_rows(grad_buffer[expert], dp_group), outer_low[slot], group_rows(activity, dp_group), group_rows(gate_proj, dp_group), group_rows(up_proj, dp_group))
                total_inner = total_inner + lax.optimization_barrier(grad_inner.astype(jnp.bfloat16)).astype(jnp.float32)
                total_outer = total_outer + lax.optimization_barrier(grad_outer.astype(jnp.bfloat16)).astype(jnp.float32)
            inner_list.append(total_inner)
            outer_list.append(total_outer)
    return (jnp.stack(inner_list), jnp.stack(outer_list))

def adam_step(weight, mean, square, grads):
    mean_new = (beta_one * mean.astype(jnp.float32) + (1.0 - beta_one) * grads).astype(jnp.bfloat16)
    square_new = (beta_two * square.astype(jnp.float32) + (1.0 - beta_two) * grads * grads).astype(jnp.bfloat16)
    mean_wide = lax.optimization_barrier(mean_new).astype(jnp.float32)
    square_wide = lax.optimization_barrier(square_new).astype(jnp.float32)
    update = mean_wide / bias_one / (jnp.sqrt(square_wide / bias_two) + adam_eps)
    return (weight - learn_rate * update, mean_new, square_new)

def reference(tokens, cotangent, norm_gain, first_ids, first_gates, second_ids, second_gates, new_slot, inner_weight, outer_weight, inner_mean, outer_mean, inner_square, outer_square):
    first_list = []
    inner_grads = []
    outer_grads = []
    for section in range(N_PIPE):
        inner_low = inner_weight[section].astype(jnp.bfloat16)
        outer_low = outer_weight[section].astype(jnp.bfloat16)
        section_out, buffer, stored = section_forward(tokens[section], norm_gain[section], first_ids[section], first_gates[section], inner_low, outer_low)
        grad_inner, grad_outer = section_grads(buffer, stored, cotangent[section], first_ids[section], first_gates[section], outer_low)
        first_list.append(section_out)
        inner_grads.append(grad_inner)
        outer_grads.append(grad_outer)
    first_out = lax.optimization_barrier(jnp.stack(first_list))
    second_in = jnp.roll(first_out, 1, axis=0)
    inner_new, inner_mean_new, inner_square_new = adam_step(inner_weight, inner_mean, inner_square, jnp.stack(inner_grads))
    outer_new, outer_mean_new, outer_square_new = adam_step(outer_weight, outer_mean, outer_square, jnp.stack(outer_grads))
    second_list = []
    for section in range(N_PIPE):
        section_out, buffer, stored = section_forward(second_in[section], norm_gain[section], second_ids[section], second_gates[section], inner_new[section].astype(jnp.bfloat16), outer_new[section].astype(jnp.bfloat16))
        second_list.append(section_out)
    layer_out = jnp.stack(second_list)
    sources = []
    halves = jnp.arange(2 * EXPERTS, dtype=jnp.int32)
    for section in range(N_PIPE):
        inverse = jnp.zeros((EXPERTS,), jnp.int32).at[new_slot[section]].set(jnp.arange(EXPERTS, dtype=jnp.int32))
        sources.append((2 * inverse[halves // 2] + halves % 2).astype(jnp.int32))

    def placed(array):
        return jnp.stack([array[section][sources[section]] for section in range(N_PIPE)])
    return (layer_out, placed(inner_new), placed(outer_new), placed(inner_mean_new), placed(outer_mean_new), placed(inner_square_new), placed(outer_square_new))
```

```python
import jax
import jax.numpy as jnp
from jax import lax
from jax.sharding import PartitionSpec as P

norm_eps = 1e-06
learn_rate = 0.001
beta_one = 0.9
beta_two = 0.95
adam_eps = 1e-08
bias_one = 0.999973438601112
bias_two = 0.994079470779667

F32 = jnp.float32
BF16 = jnp.bfloat16


def contract(left, right, left_dim, right_dim):
    return lax.dot_general(
        left, right, (((left_dim,), (right_dim,)), ((), ())), preferred_element_type=F32
    )


def normed(values, gain_row):
    widened = values.astype(F32)
    inverse_rms = lax.rsqrt(jnp.mean(widened * widened, axis=-1, keepdims=True) + norm_eps)
    return (widened * inverse_rms * gain_row).astype(BF16)


def silu_parts(gate_proj):
    logistic = jax.nn.sigmoid(gate_proj)
    return (gate_proj * logistic, logistic * (1.0 + gate_proj * (1.0 - logistic)))


def along_chips(block, distance):
    size = lax.axis_size("expert")
    return lax.ppermute(block, "expert", [(i, (i + 2 * distance) % size) for i in range(size)])


def from_sibling(block):
    return lax.ppermute(block, "expert", [(i, i ^ 1) for i in range(lax.axis_size("expert"))])


def send_blocks(blocks, sign):
    return [blocks[0]] + [along_chips(b, sign * k) for k, b in enumerate(blocks) if k]


def same_core_exchange(array):
    size = lax.axis_size("expert")
    groups = [list(range(core, size, 2)) for core in range(2)]
    return lax.all_to_all(
        array, "expert", split_axis=0, concat_axis=0, tiled=True, axis_index_groups=groups
    )


def route(ids, chip, experts, rows):
    tokens = ids.shape[0]
    names = jnp.arange(experts, dtype=jnp.int32)[None, :]
    hits = [ids[:, k : k + 1] == names for k in range(ids.shape[1])]
    named = sum(h.astype(F32) for h in hits).astype(BF16)
    earlier = (
        lax.broadcasted_iota(jnp.int32, (tokens, tokens), 1)
        < lax.broadcasted_iota(jnp.int32, (tokens, tokens), 0)
    ).astype(BF16)
    ranks = jnp.dot(earlier, named, preferred_element_type=F32)
    slots = []
    for k, hit in enumerate(hits):
        rank = jnp.sum(jnp.where(hit, ranks, 0.0), axis=1, keepdims=True).astype(jnp.int32)
        slots.append((((ids[:, k : k + 1] - chip) % experts), rank))
    return slots


def spots(slots, stride, total, offset=0):
    places = lax.broadcasted_iota(jnp.int32, (1, total), 1)
    return [places == block * stride + (rank + offset) for block, rank in slots]


def two_parts(gates):
    high = lax.reduce_precision(gates, 8, 7)
    return (high, gates - high)


def weighted(hits, gates):
    return sum(jnp.where(h, gates[:, k : k + 1], 0.0) for k, h in enumerate(hits)).astype(BF16)


def expert_forward(rows, full):
    gate_proj = contract(rows, full[0], 1, 0)
    up_proj = contract(rows, full[1], 1, 0)
    activity = (silu_parts(gate_proj)[0] * up_proj).astype(BF16)
    half_out = contract(activity, full[2], 1, 1).astype(BF16)
    return (half_out, activity, gate_proj, up_proj)


def send_back(half_out, blocks):
    here = half_out.shape[0] // 2
    other = from_sibling(half_out[here:])
    total = (half_out[:here].astype(F32) + other.astype(F32)).astype(BF16)
    rows = here // blocks
    return jnp.concatenate(
        send_blocks([total[k * rows : (k + 1) * rows] for k in range(blocks)], -1), axis=0
    )


def combine(token_rows, hits, gates, returned):
    high, low = two_parts(gates)
    mixed = jnp.dot(weighted(hits, high), returned, preferred_element_type=F32)
    mixed = mixed + jnp.dot(weighted(hits, low), returned, preferred_element_type=F32)
    return (token_rows.astype(F32) + mixed).astype(BF16)


def adam_step(weight, mean, square, grads):
    mean_new = (beta_one * mean.astype(F32) + (1.0 - beta_one) * grads).astype(BF16)
    square_new = (beta_two * square.astype(F32) + (1.0 - beta_two) * grads * grads).astype(BF16)
    mean_wide = lax.optimization_barrier(mean_new).astype(F32)
    square_wide = lax.optimization_barrier(square_new).astype(F32)
    update = mean_wide / bias_one / (jnp.sqrt(square_wide / bias_two) + adam_eps)
    return ((weight - learn_rate * update).astype(BF16), mean_new, square_new)


def full_weights(inner_low, outer_low):
    both = jnp.concatenate([inner_low, outer_low.T[None]], axis=0)
    return lax.all_gather(both, "dp", axis=1, tiled=True)


def relocate(spread, inverse):
    arrived = same_core_exchange(spread)
    ordered = jnp.concatenate(
        [lax.dynamic_slice_in_dim(arrived, inverse[i], 1, 0) for i in range(inverse.shape[0])],
        axis=0,
    )
    return same_core_exchange(ordered)


def per_device(
    tokens,
    cotangent,
    norm_gain,
    first_ids,
    first_gates,
    second_ids,
    second_gates,
    new_slot,
    inner_weight,
    outer_weight,
    inner_mean,
    outer_mean,
    inner_square,
    outer_square,
):
    experts = new_slot.shape[1]
    rows_here, width = tokens.shape[1:]
    usual = rows_here * first_ids.shape[2] // experts
    capacity = min(rows_here, usual + usual // 8)
    rows = -(-capacity // 8) * 8
    total = experts * rows
    chip = lax.axis_index("expert") // 2
    gain_row = norm_gain[0]
    x, cot = tokens[0], cotangent[0]
    w_in, w_out = inner_weight[0, 0], outer_weight[0, 0]

    full = full_weights(w_in.astype(BF16), w_out.astype(BF16))

    slots = route(first_ids[0], chip, experts, rows)
    gates = first_gates[0]
    high, low = two_parts(gates)
    one = jnp.ones_like(gates)
    picker = jnp.concatenate(
        [
            weighted(spots(slots, 2 * rows, 2 * total), one),
            weighted(spots(slots, 2 * rows, 2 * total, rows), high),
            weighted(spots(slots, 2 * rows, 2 * total, rows), low),
        ],
        axis=0,
    )
    sources = jnp.concatenate([normed(x, gain_row), cot, cot], axis=0)
    packed = contract(picker, sources, 0, 0).astype(BF16)
    sent = send_blocks([packed[2 * k * rows : 2 * (k + 1) * rows] for k in range(experts)], 1)
    own = jnp.stack(sent)
    both = jnp.stack([own, from_sibling(own)])
    arrived = both[:, :, :rows].reshape(2 * total, width)
    grad_rows = both[:, :, rows:].reshape(2 * total, width)

    half_out, activity, gate_proj, up_proj = expert_forward(arrived, full)
    hits = spots(slots, rows, total)
    first_out = combine(x, hits, gates, send_back(half_out, experts))
    second_in = lax.ppermute(
        first_out,
        "pipe",
        [(i, (i + 1) % lax.axis_size("pipe")) for i in range(lax.axis_size("pipe"))],
    )

    parts = lax.axis_size("dp")
    grad_outer = contract(grad_rows, activity, 0, 0).astype(BF16)
    sum_outer = lax.psum_scatter(grad_outer, "dp", tiled=True)
    d_active = contract(grad_rows, full[2], 1, 0)
    swish_value, swish_slope = silu_parts(gate_proj)
    d_gate = (d_active * up_proj * swish_slope).astype(BF16)
    d_upper = (d_active * swish_value).astype(BF16)
    grad_inner = jnp.stack(
        [
            contract(arrived, d, 0, 0).astype(BF16).reshape(parts, width // parts, -1)
            for d in (d_gate, d_upper)
        ],
        axis=1,
    )
    sum_inner = lax.psum_scatter(grad_inner.reshape(2 * width, -1), "dp", tiled=True)

    new_outer = adam_step(w_out, outer_mean[0, 0], outer_square[0, 0], sum_outer.astype(F32).T)
    new_inner = adam_step(
        w_in, inner_mean[0, 0], inner_square[0, 0], sum_inner.astype(F32).reshape(w_in.shape)
    )

    places = jnp.arange(experts, dtype=jnp.int32)
    inverse = jnp.sum(
        jnp.where(new_slot[0][:, None] == places[None, :], places[:, None], 0), axis=0
    )
    hidden = w_out.shape[0]
    deep = w_in.shape[1]
    spread_outer = jnp.stack([a.reshape(experts, hidden // experts, -1) for a in new_outer], axis=1)
    moved_outer = relocate(spread_outer, inverse)
    spread_inner = jnp.stack(
        [
            a.reshape(2, experts, deep // experts, hidden).transpose(1, 0, 2, 3)
            for a in new_inner
        ],
        axis=1,
    )
    moved_inner = relocate(spread_inner, inverse)
    outs_outer = [moved_outer[:, i].reshape(outer_mean.shape) for i in range(3)]
    outs_inner = [
        moved_inner[:, i].transpose(1, 0, 2, 3).reshape(inner_mean.shape) for i in range(3)
    ]

    full_two = full_weights(new_inner[0], new_outer[0])
    slots_two = route(second_ids[0], chip, experts, rows)
    hits_two = spots(slots_two, rows, total)
    picker_two = weighted(hits_two, jnp.ones_like(second_gates[0]))
    packed_two = contract(picker_two, normed(second_in, gain_row), 0, 0).astype(BF16)
    own_two = jnp.concatenate(
        send_blocks([packed_two[k * rows : (k + 1) * rows] for k in range(experts)], 1), axis=0
    )
    rows_two = jnp.concatenate([own_two, from_sibling(own_two)], axis=0)
    half_two = expert_forward(rows_two, full_two)[0]
    second_out = combine(second_in, hits_two, second_gates[0], send_back(half_two, experts))
    return (
        second_out[None],
        outs_inner[0].astype(F32),
        outs_outer[0].astype(F32),
        outs_inner[1],
        outs_outer[1],
        outs_inner[2],
        outs_outer[2],
    )


def solution(mesh):
    rows = P("pipe", ("expert", "dp"), None)
    inner = P("pipe", "expert", None, "dp", None)
    outer = P("pipe", "expert", None, "dp")
    section = P("pipe", None)
    return jax.shard_map(
        per_device,
        mesh=mesh,
        in_specs=(rows, rows, section, rows, rows, rows, rows, section)
        + (inner, outer) * 3,
        out_specs=(rows,) + (inner, outer) * 3,
        check_vma=False,
    )
```

```python
import jax
import jax.numpy as jnp
from jax import lax
from jax.experimental import pallas as pl
from jax.experimental.pallas import tpu as pltpu
from jax.sharding import PartitionSpec as P

norm_eps = 1e-06
learn_rate = 0.001
beta_one = 0.9
beta_two = 0.95
adam_eps = 1e-08
bias_one = 0.999973438601112
bias_two = 0.994079470779667

F32 = jnp.float32
BF16 = jnp.bfloat16


def contract(left, right, left_dim, right_dim):
    return lax.dot_general(
        left, right, (((left_dim,), (right_dim,)), ((), ())), preferred_element_type=F32
    )


def normed(values, gain_row):
    widened = values.astype(F32)
    inverse_rms = lax.rsqrt(jnp.mean(widened * widened, axis=-1, keepdims=True) + norm_eps)
    return (widened * inverse_rms * gain_row).astype(BF16)


def silu_parts(gate_proj):
    logistic = jax.nn.sigmoid(gate_proj)
    return (gate_proj * logistic, logistic * (1.0 + gate_proj * (1.0 - logistic)))


def along_chips(block, distance):
    size = lax.axis_size("expert")
    return lax.ppermute(block, "expert", [(i, (i + 2 * distance) % size) for i in range(size)])


def from_sibling(block):
    return lax.ppermute(block, "expert", [(i, i ^ 1) for i in range(lax.axis_size("expert"))])


def send_blocks(blocks, sign):
    count = len(blocks)
    moved = {0: blocks[0]}
    for near in range(1, count // 2 + 1):
        for k in sorted({near, count - near}):
            moved[k] = along_chips(blocks[k], sign * k)
    return [moved[k] for k in range(count)]


def same_core_exchange(array):
    size = lax.axis_size("expert")
    groups = [list(range(core, size, 2)) for core in range(2)]
    return lax.all_to_all(
        array, "expert", split_axis=0, concat_axis=0, tiled=True, axis_index_groups=groups
    )


def route(ids, chip, experts, rows):
    tokens = ids.shape[0]
    names = jnp.arange(experts, dtype=jnp.int32)[None, :]
    hits = [ids[:, k : k + 1] == names for k in range(ids.shape[1])]
    named = sum(h.astype(F32) for h in hits).astype(BF16)
    earlier = (
        lax.broadcasted_iota(jnp.int32, (tokens, tokens), 1)
        < lax.broadcasted_iota(jnp.int32, (tokens, tokens), 0)
    ).astype(BF16)
    ranks = jnp.dot(earlier, named, preferred_element_type=F32)
    slots = []
    for k, hit in enumerate(hits):
        rank = jnp.sum(jnp.where(hit, ranks, 0.0), axis=1, keepdims=True).astype(jnp.int32)
        slots.append((((ids[:, k : k + 1] - chip) % experts), rank))
    return slots


def spots(slots, stride, total, offset=0):
    places = lax.broadcasted_iota(jnp.int32, (1, total), 1)
    return [places == block * stride + (rank + offset) for block, rank in slots]


def two_parts(gates):
    high = lax.reduce_precision(gates, 8, 7)
    return (high, gates - high)


def weighted(hits, gates):
    return sum(jnp.where(h, gates[:, k : k + 1], 0.0) for k, h in enumerate(hits)).astype(BF16)


def expert_forward(rows, full):
    gate_proj = contract(rows, full[0], 1, 0)
    up_proj = contract(rows, full[1], 1, 0)
    activity = (silu_parts(gate_proj)[0] * up_proj).astype(BF16)
    half_out = contract(activity, full[2], 1, 1).astype(BF16)
    return (half_out, activity, gate_proj, up_proj)


def in_blocks(array, count):
    rows = array.shape[0] // count
    return [array[k * rows : (k + 1) * rows] for k in range(count)]


def in_step(arrays, blocks, names):
    tied = lax.optimization_barrier((*arrays, *[blocks[k] for k in names]))
    for k, block in zip(names, tied[len(arrays) :]):
        blocks[k] = block
    return tied[: len(arrays)]


def both_cores(blocks):
    own = jnp.concatenate(blocks, axis=0)
    return jnp.concatenate([own, from_sibling(own)], axis=0)


def merged_halves(half_out):
    here = half_out.shape[0] // 2
    other = from_sibling(half_out[here:])
    return (half_out[:here].astype(F32) + other.astype(F32)).astype(BF16)


def combine(token_rows, hits, gates, returned):
    high, low = two_parts(gates)
    mixed = jnp.dot(weighted(hits, high), returned, preferred_element_type=F32)
    mixed = mixed + jnp.dot(weighted(hits, low), returned, preferred_element_type=F32)
    return (token_rows.astype(F32) + mixed).astype(BF16)


def adam_step(weight, mean, square, grads):
    grads = grads.astype(F32)
    mean_new = (beta_one * mean.astype(F32) + (1.0 - beta_one) * grads).astype(BF16)
    square_new = (beta_two * square.astype(F32) + (1.0 - beta_two) * grads * grads).astype(BF16)
    mean_wide = lax.optimization_barrier(mean_new).astype(F32)
    square_wide = lax.optimization_barrier(square_new).astype(F32)
    update = mean_wide / bias_one / (jnp.sqrt(square_wide / bias_two) + adam_eps)
    return ((weight - learn_rate * update).astype(BF16), mean_new, square_new)


def side_by_side(inner, outer):
    return jnp.concatenate([inner, outer.T[None]], axis=0)


def in_eighths(array, count):
    kinds, deep, hidden = array.shape
    pieces = array.reshape(kinds, count, deep // count, hidden).transpose(1, 0, 2, 3)
    return pieces.reshape(count, kinds * (deep // count), hidden)


def from_eighths(pieces, kinds):
    count, rows, hidden = pieces.shape
    array = pieces.reshape(count, kinds, rows // kinds, hidden).transpose(1, 0, 2, 3)
    return array.reshape(kinds, count * (rows // kinds), hidden)


def full_weights(low):
    return lax.all_gather(low, "dp", axis=1, tiled=True)


def order_kernel(order_ref, inner_ref, outer_ref, out_ref):
    deep = inner_ref.shape[2]
    out_ref[:, :, :deep] = inner_ref[...]
    out_ref[:, :, deep:] = outer_ref[...]


def in_order(inner, outer, order):
    count, items, deep, hidden = inner.shape
    rows = deep + outer.shape[2]

    def block(rows):
        return pl.BlockSpec((1, items, rows, hidden), lambda i, order: (order[i], 0, 0, 0))

    return pl.pallas_call(
        order_kernel,
        grid_spec=pltpu.PrefetchScalarGridSpec(
            num_scalar_prefetch=1,
            grid=(count,),
            in_specs=[block(deep), block(rows - deep)],
            out_specs=pl.BlockSpec((1, items, rows, hidden), lambda i, order: (i, 0, 0, 0)),
        ),
        out_shape=jax.ShapeDtypeStruct((count, items, rows, hidden), inner.dtype),
        cost_estimate=pl.CostEstimate(
            flops=0, bytes_accessed=4 * count * items * rows * hidden, transcendentals=0
        ),
        name="in_order",
    )(order, inner, outer)


def per_device(
    tokens,
    cotangent,
    norm_gain,
    first_ids,
    first_gates,
    second_ids,
    second_gates,
    new_slot,
    inner_weight,
    outer_weight,
    inner_mean,
    outer_mean,
    inner_square,
    outer_square,
):
    experts = new_slot.shape[1]
    rows_here, width = tokens.shape[1:]
    usual = rows_here * first_ids.shape[2] // experts
    capacity = min(rows_here, usual + usual // 8)
    rows = -(-capacity // 8) * 8
    total = experts * rows
    chip = lax.axis_index("expert") // 2
    gain_row = norm_gain[0]
    x, cot = tokens[0], cotangent[0]
    w_in, w_out = inner_weight[0, 0], outer_weight[0, 0]

    hidden = w_out.shape[0]
    parts = lax.axis_size("dp")
    weight = side_by_side(w_in, w_out)
    mean = side_by_side(inner_mean[0, 0], outer_mean[0, 0])
    square = side_by_side(inner_square[0, 0], outer_square[0, 0])
    kinds = weight.shape[0]

    full = full_weights(weight.astype(BF16))

    slots = route(first_ids[0], chip, experts, rows)
    gates = first_gates[0]
    high, low = two_parts(gates)
    picker = jnp.concatenate(
        [
            weighted(spots(slots, 2 * rows, 2 * total), jnp.ones_like(gates)),
            weighted(spots(slots, 2 * rows, 2 * total, rows), high),
            weighted(spots(slots, 2 * rows, 2 * total, rows), low),
        ],
        axis=0,
    )
    sources = jnp.concatenate([normed(x, gain_row), cot, cot], axis=0)
    packed = contract(picker, sources, 0, 0).astype(BF16)
    own = jnp.stack(send_blocks(in_blocks(packed, experts), 1))

    both = jnp.stack([own, from_sibling(own)])
    arrived = both[:, :, :rows].reshape(2 * total, width)
    grad_rows = both[:, :, rows:].reshape(2 * total, width)
    half_out, activity, gate_proj, up_proj = expert_forward(arrived, full)

    leaving = in_blocks(merged_halves(half_out), experts)
    grad_rows, at_home = lax.optimization_barrier((grad_rows, leaving[0]))
    returned = send_blocks(leaving, -1)
    returned[0] = at_home
    hits = spots(slots, rows, total)
    grad_outer = contract(grad_rows, activity, 0, 0).astype(BF16)
    sum_outer = lax.psum_scatter(grad_outer, "dp", tiled=True)
    d_active = contract(grad_rows, full[2], 1, 0)
    swish_value, swish_slope = silu_parts(gate_proj)
    d_gate = (d_active * up_proj * swish_slope).astype(BF16)
    d_upper = (d_active * swish_value).astype(BF16)
    grad_inner = jnp.stack(
        [
            contract(arrived, d, 0, 0).astype(BF16).reshape(parts, width // parts, -1)
            for d in (d_gate, d_upper)
        ],
        axis=1,
    )
    sum_inner = lax.psum_scatter(grad_inner.reshape(2 * width, -1), "dp", tiled=True)
    hits = spots(slots, rows, total)
    first_out = combine(x, hits, gates, jnp.concatenate(returned, axis=0))
    second_in = lax.ppermute(
        first_out,
        "pipe",
        [(i, (i + 1) % lax.axis_size("pipe")) for i in range(lax.axis_size("pipe"))],
    )

    old = (weight, mean, square)
    new_outer = adam_step(*[a[2:] for a in old], sum_outer[None])
    outer_pieces = same_core_exchange(
        jnp.stack([in_eighths(a, experts) for a in new_outer], axis=1)
    )
    sum_inner, outer_pieces, second_rest = lax.optimization_barrier(
        (sum_inner, outer_pieces, second_in)
    )
    new_inner = adam_step(*[a[:2] for a in old], sum_inner.reshape(2, width // parts, hidden))
    inner_pieces = same_core_exchange(
        jnp.stack([in_eighths(a, experts) for a in new_inner], axis=1)
    )
    full_two = full_weights(jnp.concatenate([new_inner[0], new_outer[0]], axis=0))

    slots_two = route(second_ids[0], chip, experts, rows)
    hits_two = spots(slots_two, rows, total)
    picker_two = weighted(hits_two, jnp.ones_like(second_gates[0]))
    packed_two = contract(picker_two, normed(second_in, gain_row), 0, 0).astype(BF16)
    own_two = send_blocks(in_blocks(packed_two, experts), 1)

    places = jnp.arange(experts, dtype=jnp.int32)
    inverse = jnp.sum(
        jnp.where(new_slot[0][:, None] == places[None, :], places[:, None], 0), axis=0
    )
    ordered = in_order(inner_pieces, outer_pieces, inverse)
    (ordered,) = in_step([ordered], own_two, range(1, experts))
    moved = same_core_exchange(ordered)

    half_two = expert_forward(both_cores(own_two), full_two)[0]
    leaving_two = in_blocks(merged_halves(half_two), experts)
    returned_two = send_blocks(leaving_two, -1)
    (moved,) = in_step([moved], returned_two, (1, 2, experts - 2, experts - 1))
    second_out = combine(
        second_rest, hits_two, second_gates[0], jnp.concatenate(returned_two, axis=0)
    )
    outs = []
    for item in range(moved.shape[1]):
        array = from_eighths(moved[:, item], kinds)
        outs += [array[:-1].reshape(inner_mean.shape), array[-1].T.reshape(outer_mean.shape)]
    return (second_out[None], outs[0].astype(F32), outs[1].astype(F32), *outs[2:])


def solution(mesh):
    rows = P("pipe", ("expert", "dp"), None)
    inner = P("pipe", "expert", None, "dp", None)
    outer = P("pipe", "expert", None, "dp")
    section = P("pipe", None)
    return jax.shard_map(
        per_device,
        mesh=mesh,
        in_specs=(rows, rows, section, rows, rows, rows, rows, section)
        + (inner, outer) * 3,
        out_specs=(rows,) + (inner, outer) * 3,
        check_vma=False,
    )
```

```python
import jax
import jax.numpy as jnp
from jax import lax
from jax.experimental import pallas as pl
from jax.experimental.pallas import tpu as pltpu
from jax.sharding import PartitionSpec as P

norm_eps = 1e-06
learn_rate = 0.001
beta_one = 0.9
beta_two = 0.95
adam_eps = 1e-08
bias_one = 0.999973438601112
bias_two = 0.994079470779667

F32 = jnp.float32
BF16 = jnp.bfloat16


def contract(left, right, left_dim, right_dim):
    return lax.dot_general(
        left, right, (((left_dim,), (right_dim,)), ((), ())), preferred_element_type=F32
    )


def normed(values, gain_row):
    widened = values.astype(F32)
    inverse_rms = lax.rsqrt(jnp.mean(widened * widened, axis=-1, keepdims=True) + norm_eps)
    return (widened * inverse_rms * gain_row).astype(BF16)


def silu_parts(gate_proj):
    logistic = jax.nn.sigmoid(gate_proj)
    return (gate_proj * logistic, logistic * (1.0 + gate_proj * (1.0 - logistic)))


def along_chips(block, distance):
    size = lax.axis_size("expert")
    return lax.ppermute(block, "expert", [(i, (i + 2 * distance) % size) for i in range(size)])


def from_sibling(block):
    return lax.ppermute(block, "expert", [(i, i ^ 1) for i in range(lax.axis_size("expert"))])


def send_blocks(blocks, sign):
    count = len(blocks)
    moved = {0: blocks[0]}
    for near in range(1, count // 2 + 1):
        for k in sorted({near, count - near}):
            moved[k] = along_chips(blocks[k], sign * k)
    return [moved[k] for k in range(count)]


def same_core_exchange(array):
    size = lax.axis_size("expert")
    groups = [list(range(core, size, 2)) for core in range(2)]
    return lax.all_to_all(
        array, "expert", split_axis=0, concat_axis=0, tiled=True, axis_index_groups=groups
    )


def route(ids, chip, experts, rows):
    tokens = ids.shape[0]
    names = jnp.arange(experts, dtype=jnp.int32)[None, :]
    hits = [ids[:, k : k + 1] == names for k in range(ids.shape[1])]
    named = sum(h.astype(F32) for h in hits).astype(BF16)
    earlier = (
        lax.broadcasted_iota(jnp.int32, (tokens, tokens), 1)
        < lax.broadcasted_iota(jnp.int32, (tokens, tokens), 0)
    ).astype(BF16)
    ranks = jnp.dot(earlier, named, preferred_element_type=F32)
    slots = []
    for k, hit in enumerate(hits):
        rank = jnp.sum(jnp.where(hit, ranks, 0.0), axis=1, keepdims=True).astype(jnp.int32)
        slots.append((((ids[:, k : k + 1] - chip) % experts), rank))
    return slots


def spots(slots, stride, total, offset=0):
    places = lax.broadcasted_iota(jnp.int32, (1, total), 1)
    return [places == block * stride + (rank + offset) for block, rank in slots]


def two_parts(gates):
    high = lax.reduce_precision(gates, 8, 7)
    return (high, gates - high)


def weighted(hits, gates):
    return sum(jnp.where(h, gates[:, k : k + 1], 0.0) for k, h in enumerate(hits)).astype(BF16)


def expert_forward(rows, full):
    gate_proj = contract(rows, full[0], 1, 0)
    up_proj = contract(rows, full[1], 1, 0)
    activity = (silu_parts(gate_proj)[0] * up_proj).astype(BF16)
    half_out = contract(activity, full[2], 1, 1).astype(BF16)
    return (half_out, activity, gate_proj, up_proj)


def in_blocks(array, count):
    rows = array.shape[0] // count
    return [array[k * rows : (k + 1) * rows] for k in range(count)]


def in_step(arrays, blocks, names):
    tied = lax.optimization_barrier((*arrays, *[blocks[k] for k in names]))
    for k, block in zip(names, tied[len(arrays) :]):
        blocks[k] = block
    return tied[: len(arrays)]


def both_cores(blocks):
    own = jnp.concatenate(blocks, axis=0)
    return jnp.concatenate([own, from_sibling(own)], axis=0)


def merged_halves(half_out):
    here = half_out.shape[0] // 2
    other = from_sibling(half_out[here:])
    return (half_out[:here].astype(F32) + other.astype(F32)).astype(BF16)


def combine(token_rows, hits, gates, returned):
    high, low = two_parts(gates)
    mixed = jnp.dot(weighted(hits, high), returned, preferred_element_type=F32)
    mixed = mixed + jnp.dot(weighted(hits, low), returned, preferred_element_type=F32)
    return (token_rows.astype(F32) + mixed).astype(BF16)


def step_kernel(weight_ref, mean_ref, square_ref, grad_ref, out_ref, low_ref):
    rows = out_ref.shape[3]
    for piece in range(out_ref.shape[0]):
        here = (slice(None), slice(piece * rows, (piece + 1) * rows))
        grads = grad_ref[here].astype(F32)
        mean_new = (beta_one * mean_ref[here].astype(F32) + (1.0 - beta_one) * grads).astype(BF16)
        square_new = beta_two * square_ref[here].astype(F32) + (1.0 - beta_two) * grads * grads
        square_new = square_new.astype(BF16)
        root = jnp.sqrt(square_new.astype(F32) * (1.0 / bias_two)) + adam_eps
        update = mean_new.astype(F32) * (learn_rate / bias_one) / root
        low = (weight_ref[here] - update).astype(BF16)
        out_ref[piece, 0] = low
        out_ref[piece, 1] = mean_new
        out_ref[piece, 2] = square_new
        low_ref[here] = low


def stepped_eighths(weight, mean, square, grads, count):
    kinds, deep, hidden = weight.shape
    rows = deep // count
    each = 2
    here = pl.BlockSpec((kinds, each * rows, hidden), lambda i: (0, i, 0))
    pieces, low = pl.pallas_call(
        step_kernel,
        grid=(count // each,),
        in_specs=[here] * 4,
        out_specs=[pl.BlockSpec((each, 3, kinds, rows, hidden), lambda i: (i, 0, 0, 0, 0)), here],
        out_shape=[
            jax.ShapeDtypeStruct((count, 3, kinds, rows, hidden), BF16),
            jax.ShapeDtypeStruct(weight.shape, BF16),
        ],
        cost_estimate=pl.CostEstimate(
            flops=16 * weight.size, bytes_accessed=18 * weight.size, transcendentals=2 * weight.size
        ),
        name="stepped_eighths",
    )(weight, mean, square, grads)
    return (pieces.reshape(count, 3, kinds * rows, hidden), low)


def side_by_side(inner, outer):
    return jnp.concatenate([inner, outer.T[None]], axis=0)


def from_eighths(pieces, kinds):
    count, rows, hidden = pieces.shape
    array = pieces.reshape(count, kinds, rows // kinds, hidden).transpose(1, 0, 2, 3)
    return array.reshape(kinds, count * (rows // kinds), hidden)


def full_weights(low):
    return lax.all_gather(low, "dp", axis=1, tiled=True)


def order_kernel(order_ref, inner_ref, outer_ref, out_ref):
    deep = inner_ref.shape[2]
    out_ref[:, :, :deep] = inner_ref[...]
    out_ref[:, :, deep:] = outer_ref[...]


def in_order(inner, outer, order):
    count, items, deep, hidden = inner.shape
    rows = deep + outer.shape[2]

    def block(rows):
        return pl.BlockSpec((1, items, rows, hidden), lambda i, order: (order[i], 0, 0, 0))

    return pl.pallas_call(
        order_kernel,
        grid_spec=pltpu.PrefetchScalarGridSpec(
            num_scalar_prefetch=1,
            grid=(count,),
            in_specs=[block(deep), block(rows - deep)],
            out_specs=pl.BlockSpec((1, items, rows, hidden), lambda i, order: (i, 0, 0, 0)),
        ),
        out_shape=jax.ShapeDtypeStruct((count, items, rows, hidden), inner.dtype),
        cost_estimate=pl.CostEstimate(
            flops=0, bytes_accessed=4 * count * items * rows * hidden, transcendentals=0
        ),
        name="in_order",
    )(order, inner, outer)


def per_device(
    tokens,
    cotangent,
    norm_gain,
    first_ids,
    first_gates,
    second_ids,
    second_gates,
    new_slot,
    inner_weight,
    outer_weight,
    inner_mean,
    outer_mean,
    inner_square,
    outer_square,
):
    experts = new_slot.shape[1]
    rows_here, width = tokens.shape[1:]
    usual = rows_here * first_ids.shape[2] // experts
    capacity = min(rows_here, usual + usual // 8)
    rows = -(-capacity // 8) * 8
    total = experts * rows
    chip = lax.axis_index("expert") // 2
    gain_row = norm_gain[0]
    x, cot = tokens[0], cotangent[0]
    w_in, w_out = inner_weight[0, 0], outer_weight[0, 0]

    hidden = w_out.shape[0]
    parts = lax.axis_size("dp")
    weight = side_by_side(w_in, w_out)
    kinds = weight.shape[0]

    full = full_weights(weight.astype(BF16))

    slots = route(first_ids[0], chip, experts, rows)
    gates = first_gates[0]
    high, low = two_parts(gates)
    picker = jnp.concatenate(
        [
            weighted(spots(slots, 2 * rows, 2 * total), jnp.ones_like(gates)),
            weighted(spots(slots, 2 * rows, 2 * total, rows), high),
            weighted(spots(slots, 2 * rows, 2 * total, rows), low),
        ],
        axis=0,
    )
    sources = jnp.concatenate([normed(x, gain_row), cot, cot], axis=0)
    packed = contract(picker, sources, 0, 0).astype(BF16)
    own = jnp.stack(send_blocks(in_blocks(packed, experts), 1))

    both = jnp.stack([own, from_sibling(own)])
    arrived = both[:, :, :rows].reshape(2 * total, width)
    grad_rows = both[:, :, rows:].reshape(2 * total, width)
    half_out, activity, gate_proj, up_proj = expert_forward(arrived, full)

    leaving = in_blocks(merged_halves(half_out), experts)
    grad_rows, at_home = lax.optimization_barrier((grad_rows, leaving[0]))
    returned = send_blocks(leaving, -1)
    returned[0] = at_home
    hits = spots(slots, rows, total)
    grad_outer = contract(grad_rows, activity, 0, 0).astype(BF16)
    sum_outer = lax.psum_scatter(grad_outer, "dp", tiled=True)
    d_active = contract(grad_rows, full[2], 1, 0)
    swish_value, swish_slope = silu_parts(gate_proj)
    d_gate = (d_active * up_proj * swish_slope).astype(BF16)
    d_upper = (d_active * swish_value).astype(BF16)
    grad_inner = jnp.stack(
        [
            contract(arrived, d, 0, 0).astype(BF16).reshape(parts, width // parts, -1)
            for d in (d_gate, d_upper)
        ],
        axis=1,
    )
    sum_inner = lax.psum_scatter(grad_inner.reshape(2 * width, -1), "dp", tiled=True)
    hits = spots(slots, rows, total)
    first_out = combine(x, hits, gates, jnp.concatenate(returned, axis=0))
    second_in = lax.ppermute(
        first_out,
        "pipe",
        [(i, (i + 1) % lax.axis_size("pipe")) for i in range(lax.axis_size("pipe"))],
    )

    outer_old = [a.T[None] for a in (w_out, outer_mean[0, 0], outer_square[0, 0])]
    new_outer, low_outer = stepped_eighths(*outer_old, sum_outer[None], experts)
    outer_pieces = same_core_exchange(new_outer)
    sum_inner, outer_pieces, second_rest = lax.optimization_barrier(
        (sum_inner, outer_pieces, second_in)
    )
    new_inner, low_inner = stepped_eighths(
        w_in,
        inner_mean[0, 0],
        inner_square[0, 0],
        sum_inner.reshape(2, width // parts, hidden),
        experts,
    )
    inner_pieces = same_core_exchange(new_inner)
    full_two = full_weights(jnp.concatenate([low_inner, low_outer], axis=0))

    slots_two = route(second_ids[0], chip, experts, rows)
    hits_two = spots(slots_two, rows, total)
    picker_two = weighted(hits_two, jnp.ones_like(second_gates[0]))
    packed_two = contract(picker_two, normed(second_in, gain_row), 0, 0).astype(BF16)
    own_two = send_blocks(in_blocks(packed_two, experts), 1)

    places = jnp.arange(experts, dtype=jnp.int32)
    inverse = jnp.sum(
        jnp.where(new_slot[0][:, None] == places[None, :], places[:, None], 0), axis=0
    )
    ordered = in_order(inner_pieces, outer_pieces, inverse)
    moved = same_core_exchange(ordered)

    half_two = expert_forward(both_cores(own_two), full_two)[0]
    leaving_two = in_blocks(merged_halves(half_two), experts)
    returned_two = send_blocks(leaving_two, -1)
    (moved,) = in_step([moved], returned_two, (1, 2, experts - 2, experts - 1))
    second_out = combine(
        second_rest, hits_two, second_gates[0], jnp.concatenate(returned_two, axis=0)
    )
    outs = []
    for item in range(moved.shape[1]):
        array = from_eighths(moved[:, item], kinds)
        outs += [array[:-1].reshape(inner_mean.shape), array[-1].T.reshape(outer_mean.shape)]
    return (second_out[None], outs[0].astype(F32), outs[1].astype(F32), *outs[2:])


def solution(mesh):
    rows = P("pipe", ("expert", "dp"), None)
    inner = P("pipe", "expert", None, "dp", None)
    outer = P("pipe", "expert", None, "dp")
    section = P("pipe", None)
    return jax.shard_map(
        per_device,
        mesh=mesh,
        in_specs=(rows, rows, section, rows, rows, rows, rows, section)
        + (inner, outer) * 3,
        out_specs=(rows,) + (inner, outer) * 3,
        check_vma=False,
    )
```
